32 devices in a mesh: groups: 2 (over y), ctx: 4 (over z), tp: 2 (over x), dp: 2 (over core).
Axes of the slice: x: 2, y: 2, z: 4, core: 2. Of those that a mesh axis runs over, the one named last changes fastest.
Arguments:
- x_in: bfloat16 [4096, 8192], P(('groups', 'ctx', 'dp'), 'tp'), parts along dimension 0, may hold values from -6 to 6
- bc_in: bfloat16 [4096, 2, 1024], P(('groups', 'ctx', 'dp'), None, 'tp'), parts along dimension 0, may hold values from -6 to 6
- gate_z: bfloat16 [4096, 8192], P(('groups', 'ctx', 'dp'), 'tp'), parts along dimension 0, may hold values from -60 to 60
- log_decay: float32 [2, 4096, 128], P(None, ('groups', 'ctx', 'dp'), 'tp'), parts along dimension 1, may hold values from -1 to 0
- resets: int32 [4096], P(('groups', 'ctx', 'dp')), parts along dimension 0, may hold values from 0 to 1, as said below
- conv_x: float32 [4, 8192], P(None, 'tp'), may hold values from -3 to 3
- conv_bc: float32 [4, 2, 1024], P(None, None, 'tp'), may hold values from -1.8 to 1.8
- skip_d: float32 [128], P('tp'), may hold values from 0.25 to 2
- norm_gain: float32 [8192], P('tp'), may hold values from 0.5 to 1.5
- visit_span: int32 [256, 2], P(('groups', 'ctx', 'dp')), parts along dimension 0, may hold values from 0 to 2048, as said below
Outputs:
- token_out: bfloat16 [4096, 8192], P(('groups', 'ctx', 'dp'), 'tp'), parts along dimension 0
- pooled: bfloat16 [256, 8192], P(('groups', 'ctx', 'dp'), 'tp'), parts along dimension 0
The draws below stay inside these ranges and needn't reach their ends.
There are 2 independent parts, one for each index of `groups`. The reference program is written for one: setup_inputs(seed, part) draws one part's arguments, and reference() takes and returns one part's arrays. A program takes and returns all parts, laid end to end along the dimension named above; an argument that names none is the same for every part. Nothing has to cross between parts.
Inputs may be any that keep to these rules, and one draw needn't show every extreme that they name: `resets`: at most 3 tokens carry a 1, never token 0; a 1 opens a new patient stream. `visit_span`: the visits in rows k * 16 to (k + 1) * 16 - 1 begin in tokens k * 256 to (k + 1) * 256 - 1; every visit holds 1 to 256 tokens and some visit holds exactly 256; visits may intersect.
All inputs are finite; a program needn't handle non-finite values.
Results may differ from the reference program's by a relative error of at most 0.0036.
Values may be sent and summed in bfloat16 or wider, within the bound.
A program may use at most 128 MiB of HBM per device.

```python
import math
import jax
import jax.numpy as jnp
from jax import lax

HEADS = 128
HEADDIM = 64
STATE = 128
GROUPS = 8
CONV = 4
INNER = 8192
TOK_DEV = 256
STRETCH = 256
VISLEN = 256
VIS_DEV = 16
WINDOW_TOKENS = 2048
VISITS = 128


def draw_log_decay(key, part):
    key_sequence = jax.random.split(key, 7)
    fast_share = 0.5
    fast_heads = jax.random.uniform(key_sequence[0], (2, HEADS)) < fast_share
    fast_rate = jnp.exp(jax.random.uniform(key_sequence[1], (2, HEADS), minval=math.log(1.0 / 50.0), maxval=math.log(1.0 / 30.0)))
    slow_rate = jnp.exp(jax.random.uniform(key_sequence[2], (2, HEADS), minval=math.log(0.1), maxval=0.0)) / WINDOW_TOKENS
    head_decay_rate = jnp.where(fast_heads, fast_rate, slow_rate)
    block_count = WINDOW_TOKENS // TOK_DEV
    block_multiplier = jnp.exp(jax.random.uniform(key_sequence[3], (2, block_count, HEADS), minval=math.log(0.5), maxval=math.log(2.0)))
    block_multiplier = jnp.repeat(block_multiplier, TOK_DEV, axis=1)
    token_multiplier = jnp.exp(jax.random.uniform(key_sequence[4], (2, WINDOW_TOKENS, HEADS), minval=math.log(0.5), maxval=math.log(2.0)))
    spike_location = jax.random.randint(key_sequence[5], (2, 2), 0, WINDOW_TOKENS)
    spike_magnitude = jax.random.uniform(key_sequence[6], (2, 2), minval=0.22, maxval=0.69)
    token_position = jnp.arange(WINDOW_TOKENS)
    spike_penalty = jnp.sum((token_position[None, None, :] == spike_location[:, :, None]).astype(jnp.float32) * spike_magnitude[:, :, None], axis=1)
    return -(head_decay_rate[:, None, :] * block_multiplier * token_multiplier) - spike_penalty[:, :, None]


def draw_resets(key, part):
    where_at = jax.random.randint(key, (3,), 1, WINDOW_TOKENS)
    token_position = jnp.arange(WINDOW_TOKENS)
    return jnp.any(token_position[:, None] == where_at[None, :], axis=1).astype(jnp.int32)


def draw_gate_z(key, part):
    key_sequence = jax.random.split(key, 3)
    row_scale = jnp.exp(jax.random.uniform(key_sequence[0], (WINDOW_TOKENS, 1), minval=math.log(0.3), maxval=math.log(3.0)))
    col_scale = jnp.exp(jax.random.uniform(key_sequence[1], (1, INNER), minval=math.log(0.3), maxval=math.log(3.0)))
    base = jnp.clip(jax.random.normal(key_sequence[2], (WINDOW_TOKENS, INNER)), -6.0, 6.0)
    return (base * row_scale * col_scale).astype(jnp.bfloat16)


def draw_visit_span(key, part):
    key_sequence = jax.random.split(key, 3)
    index = jnp.arange(VISITS)
    owner_block = index // VIS_DEV
    span_len = jax.random.randint(key_sequence[0], (VISITS,), 1, VISLEN + 1)
    longest = jax.random.randint(key_sequence[1], (), 0, VISITS)
    span_len = jnp.where(index == longest, VISLEN, span_len)
    block_last = index % VIS_DEV == VIS_DEV - 1
    span_len = jnp.where(block_last, VISLEN, span_len)
    offset_in = jax.random.randint(key_sequence[2], (VISITS,), 0, TOK_DEV)
    offset_in = jnp.where(block_last, TOK_DEV - 1, offset_in)
    begin = jnp.minimum(owner_block * TOK_DEV + offset_in, WINDOW_TOKENS - span_len)
    begin = jnp.where(index == 0, 0, begin)
    begin = jnp.where(index == VISITS - 1, WINDOW_TOKENS - span_len, begin)
    return jnp.stack([begin, begin + span_len], axis=1).astype(jnp.int32)


def levels(key, dims, cuts, least, top_value):
    factor_of = 1.0
    for axis_at, parts in cuts:
        steps = jax.random.uniform(jax.random.fold_in(jax.random.fold_in(key, 6), axis_at), (parts,), jnp.float32, least / len(cuts), top_value / len(cuts))
        factor_of = factor_of * jnp.repeat(jnp.exp(steps), dims[axis_at] // parts).reshape((-1,) + (1,) * (len(dims) - 1 - axis_at))
    return factor_of


def gaussian(key, dims, scale, most, cuts=(), kind=jnp.bfloat16):
    result = jax.random.normal(key, dims, jnp.float32) * scale
    if len(cuts) > 0:
        result = levels(key, dims, cuts, -0.22, 0.18) * result
    return jnp.clip(result, min=-most, max=most).astype(kind)


def setup_inputs(seed: int = 0, part: int = 0) -> dict:
    seeds = jax.random.split(jax.random.key(seed), 11)
    own_keys = jax.random.split(jax.random.fold_in(seeds[10], part), 11)
    return {
        "x_in": gaussian(own_keys[0], (WINDOW_TOKENS, INNER), 1.0, 6.0, ((0, 8), (1, 2))),
        "bc_in": gaussian(own_keys[1], (WINDOW_TOKENS, 2, GROUPS * STATE), 1.0, 6.0, ((0, 8), (2, 2))),
        "gate_z": draw_gate_z(jax.random.fold_in(jax.random.fold_in(seeds[10], part), 71), part),
        "log_decay": draw_log_decay(jax.random.fold_in(jax.random.fold_in(seeds[10], part), 71), part),
        "resets": draw_resets(jax.random.fold_in(jax.random.fold_in(seeds[10], part), 71), part),
        "conv_x": gaussian(seeds[5], (CONV, INNER), 0.5, 3.0, ((1, 2),), jnp.float32),
        "conv_bc": gaussian(seeds[6], (CONV, 2, GROUPS * STATE), 0.3, 1.8, ((2, 2),), jnp.float32),
        "skip_d": jnp.clip(0.25 + 1.75 * jax.random.uniform(seeds[7], (HEADS,), jnp.float32) ** levels(seeds[7], (HEADS,), ((0, 2),), -0.2, 0.2), 0.25, 2.0),
        "norm_gain": jnp.clip(1.0 + 0.1 * jax.random.normal(seeds[8], (INNER,), jnp.float32), 0.5, 1.5),
        "visit_span": draw_visit_span(jax.random.fold_in(jax.random.fold_in(seeds[10], part), 71), part),
    }


def conv_silu(signal, rim, weight):
    kernel = weight.shape[0]
    length = signal.shape[0]
    padded = jnp.concatenate([rim, signal], axis=0).astype(jnp.float32)
    summed = weight[0] * padded[0:length]
    for offset in range(1, kernel):
        summed = summed + weight[offset] * padded[offset:offset + length]
    return jax.nn.silu(summed).astype(jnp.bfloat16)

def input_weight(log_rate):
    return jnp.sqrt(-jnp.expm1(2.0 * log_rate))

def stretch_parts(x_block, b_block, c_block, log_block, break_block, scale_block, strict):
    length = x_block.shape[0]
    per_group = x_block.shape[1] // b_block.shape[1]
    cumul = jnp.cumsum(log_block, axis=0)
    segment = jnp.cumsum(break_block)
    token_position = jnp.arange(length)
    if strict:
        ordered = token_position[:, None] > token_position[None, :]
    else:
        ordered = token_position[:, None] >= token_position[None, :]
    keeping = (ordered & (segment[:, None] == segment[None, :]))[None]
    cumul_t = cumul.T
    spread = jnp.where(keeping, cumul_t[:, :, None] - cumul_t[:, None, :], 0.0)
    decays = jnp.where(keeping, jnp.exp(spread), 0.0)
    scores = jnp.einsum('ign,jgn->gij', c_block.astype(jnp.float32), b_block.astype(jnp.float32))
    scores = jnp.repeat(scores, per_group, axis=0)
    mixing = (scores * decays * scale_block.T[:, None, :]).astype(jnp.bfloat16)
    y_inner = jnp.einsum('hij,jhp->ihp', mixing.astype(jnp.float32), x_block.astype(jnp.float32))
    same_end = (segment[-1] == segment).astype(jnp.float32)
    to_end = jnp.exp(cumul[-1][None, :] - cumul) * same_end[:, None] * scale_block
    weighted = (x_block.astype(jnp.float32) * to_end[:, :, None]).astype(jnp.bfloat16)
    b_heads = jnp.repeat(b_block, per_group, axis=1)
    stretch_state = jnp.einsum('jhp,jhn->hpn', weighted.astype(jnp.float32), b_heads.astype(jnp.float32))
    carried = jnp.exp(cumul[-1]) * (segment[-1] == 0).astype(jnp.float32)
    leading = jnp.exp(cumul) * (segment == 0).astype(jnp.float32)[:, None]
    return (y_inner, stretch_state, carried, leading)

def direction_sweep(x_heads, b_mat, c_mat, log_rate, break_flags, scales, strict):
    stretches = x_heads.shape[0] // STRETCH
    per_group = x_heads.shape[1] // b_mat.shape[1]

    def blocks(array):
        return array.reshape((stretches, STRETCH) + array.shape[1:])

    def advance(state_now, pieces):
        y_inner, stretch_state, carried, leading = stretch_parts(*pieces, strict)
        c_heads = jnp.repeat(pieces[2], per_group, axis=1).astype(jnp.float32)
        from_state = jnp.einsum('ihn,hpn->ihp', c_heads, state_now, precision=lax.Precision.HIGHEST)
        return (carried[:, None, None] * state_now + stretch_state, y_inner + leading[:, :, None] * from_state)
    initial = jnp.zeros((x_heads.shape[1], x_heads.shape[2], b_mat.shape[2]), jnp.float32)
    pieces = tuple((blocks(a) for a in (x_heads, b_mat, c_mat, log_rate, break_flags, scales)))
    _, outputs = lax.scan(advance, initial, pieces)
    return outputs.reshape(x_heads.shape)

def reference(x_in, bc_in, gate_z, log_decay, resets, conv_x, conv_bc, skip_d, norm_gain, visit_span):
    kernel = conv_x.shape[0]
    x_conv = conv_silu(x_in, jnp.zeros((kernel - 1, x_in.shape[1]), jnp.bfloat16), conv_x)
    bc_conv = conv_silu(bc_in, jnp.zeros((kernel - 1,) + bc_in.shape[1:], jnp.bfloat16), conv_bc)
    x_heads = x_conv.reshape(WINDOW_TOKENS, HEADS, HEADDIM)
    b_mat = bc_conv[:, 0].reshape(WINDOW_TOKENS, GROUPS, STATE)
    c_mat = bc_conv[:, 1].reshape(WINDOW_TOKENS, GROUPS, STATE)
    forward_log = log_decay[0]
    backward_log = log_decay[1]
    y_fwd = direction_sweep(x_heads, b_mat, c_mat, forward_log, resets, input_weight(forward_log), False)
    rev_log = jnp.concatenate([jnp.zeros((1, HEADS), jnp.float32), jnp.flip(backward_log, 0)[:-1]], axis=0)
    rev_break = jnp.concatenate([jnp.zeros((1,), jnp.int32), jnp.flip(resets, 0)[:-1]], axis=0)
    y_rev = direction_sweep(jnp.flip(x_heads, 0), jnp.flip(b_mat, 0), jnp.flip(c_mat, 0), rev_log, rev_break, jnp.flip(input_weight(backward_log), 0), True)
    mixed = y_fwd + jnp.flip(y_rev, 0) + skip_d[None, :, None] * x_heads.astype(jnp.float32)
    group_width = INNER // GROUPS
    gated = mixed.reshape(WINDOW_TOKENS, GROUPS, group_width) * jax.nn.silu(gate_z.astype(jnp.float32)).reshape(WINDOW_TOKENS, GROUPS, group_width)
    mean_sq = lax.optimization_barrier(jnp.mean(gated * gated, axis=2, keepdims=True))
    normed = (gated * lax.rsqrt(mean_sq + 1e-05)).reshape(WINDOW_TOKENS, INNER) * norm_gain
    token_out = normed.astype(jnp.bfloat16)
    token_position = jnp.arange(WINDOW_TOKENS)
    inside = ((token_position[None, :] >= visit_span[:, 0:1]) & (token_position[None, :] < visit_span[:, 1:2])).astype(jnp.bfloat16)
    sums = jnp.dot(inside, token_out, preferred_element_type=jnp.float32)
    pooled = (sums / (visit_span[:, 1:2] - visit_span[:, 0:1]).astype(jnp.float32)).astype(jnp.bfloat16)
    return (token_out, pooled)
```

```python
import functools
import jax
import jax.numpy as jnp
from jax import lax
from jax.experimental import pallas as pl
from jax.experimental.pallas import tpu as pltpu
from jax.sharding import PartitionSpec as P

HEADDIM = 64
STATE = 128
GROUPS = 8
PER = 16
LOG2E = 1.4426950408889634
BIG = 160.0
HALO = 8
MESH = pl.DeviceIdType.MESH


def silu(v):
    return v / (1.0 + jnp.exp(-v))


def conv(rim, block, taps):
    padded = jnp.concatenate([rim.astype(jnp.float32), block.astype(jnp.float32)], axis=0)
    total = taps[3:4] * padded[HALO:]
    for k in range(3):
        total = total + taps[k : k + 1] * pltpu.roll(padded, 3 - k, 0)[HALO:]
    return silu(total).astype(jnp.bfloat16)


def dot(a, b):
    return jnp.dot(a, b, preferred_element_type=jnp.float32)


def kernel(
    chips,
    groups,
    x_ref, bc_ref, gate_ref, rate_ref, lw_ref, taps_x, taps_bc, skip_ref, gain_ref, span_ref,
    out_ref, pool_ref,
    halo_x, halo_bc, span_in, xc, bs, cs, colt, rowt, lead_hl, expand, y_acc, h_lead,
    s_own, t_own, s_send, t_send, s_in, t_in, chain_in, follow_in, chain_out,
    own_pool, spill_out, spill_in,
    sem_halo, sem_s, sem_t, sem_chain, sem_follow, sem_spill,
):
    tokens = x_ref.shape[0]
    width = PER * HEADDIM
    half = tokens // 2
    c = lax.axis_index("ctx")
    d = lax.axis_index("dp")
    other = 1 - d
    nxt = c + 2 * d - 1
    prv = c - 2 * d + 1
    pos = d * c + (1 - d) * (chips - 1 - c)
    has_next = pos < chips - 1
    has_prev = pos > 0
    index = c * 2 + d
    last_index = chips * 2 - 1
    partner = {"ctx": c, "dp": other}
    halo_to = {"ctx": d * nxt + (1 - d) * c, "dp": other}
    spill_to = {"ctx": d * c + (1 - d) * nxt, "dp": other}
    follow_chain = {"ctx": nxt, "dp": d}

    barrier = pltpu.get_barrier_semaphore()
    pl.semaphore_signal(barrier, inc=1, device_id=partner, device_id_type=MESH)

    @pl.when(has_next)
    def _():
        pl.semaphore_signal(barrier, inc=1, device_id={"ctx": nxt, "dp": other}, device_id_type=MESH)
        pl.semaphore_signal(barrier, inc=1, device_id={"ctx": nxt, "dp": d}, device_id_type=MESH)

    @pl.when(has_prev)
    def _():
        pl.semaphore_signal(barrier, inc=1, device_id={"ctx": prv, "dp": d}, device_id_type=MESH)

    pl.semaphore_wait(barrier, 1 + 2 * has_next.astype(jnp.int32) + has_prev.astype(jnp.int32))

    def remote(src, dst, sems, k, to):
        return pltpu.make_async_remote_copy(
            src_ref=src, dst_ref=dst, send_sem=sems.at[0, k], recv_sem=sems.at[1, k],
            device_id=to, device_id_type=MESH,
        )

    tail = pl.ds(tokens - HALO, HALO)
    halos = (
        remote(x_ref.at[tail], halo_x, sem_halo, 0, halo_to),
        remote(bc_ref.at[tail], halo_bc, sem_halo, 1, halo_to),
        remote(span_ref, span_in, sem_halo, 2, halo_to),
    )

    @pl.when(index < last_index)
    def _():
        for copy in halos:
            copy.start()

    def s_copy(g):
        return remote(s_send.at[g], s_in.at[g], sem_s, g, partner)

    def t_copy(g):
        return remote(t_send.at[g], t_in.at[g], sem_t, g, partner)

    def chain_copy(g):
        return remote(chain_out.at[g], chain_in.at[g], sem_chain, g, follow_chain)

    def follow_copy(g):
        return remote(chain_in.at[g], follow_in.at[g], sem_follow, g, partner)

    def spill_copy(g):
        return remote(spill_out.at[g], spill_in.at[g], sem_spill, g, spill_to)

    rows = lax.broadcasted_iota(jnp.int32, (tokens, tokens), 0)
    cols = lax.broadcasted_iota(jnp.int32, (tokens, tokens), 1)
    tri = (rows >= cols).astype(jnp.float32)
    lane = lax.broadcasted_iota(jnp.int32, (tokens, 128), 1)
    is_fwd = lane < PER
    live = lane < 2 * PER
    erow = lax.rem(lax.broadcasted_iota(jnp.int32, (128, width), 0), 2 * PER)
    ebelow = lax.broadcasted_iota(jnp.int32, (128, width), 0) < 4 * PER
    ehead = lax.div(lax.broadcasted_iota(jnp.int32, (128, width), 1), HEADDIM)
    expand[0] = ((erow == ehead + PER * (1 - d)) & ebelow).astype(jnp.float32).astype(jnp.bfloat16)
    expand[1] = ((erow == ehead + PER * d) & ebelow).astype(jnp.float32).astype(jnp.bfloat16)

    @pl.when(index == 0)
    def _():
        halo_x[...] = jnp.zeros_like(halo_x)
        halo_bc[...] = jnp.zeros_like(halo_bc)
        span_in[...] = jnp.zeros_like(span_in)

    @pl.when(index > 0)
    def _():
        for copy in halos:
            copy.wait_recv()

    def hi_lo(v):
        v = jnp.where(live[: v.shape[0]], v, 0.0)
        hi = v.astype(jnp.bfloat16).astype(jnp.float32)
        return (hi + pltpu.roll(v - hi, 2 * PER, 1)).astype(jnp.bfloat16)

    @pl.loop(0, groups)
    def _(g):
        wide = pl.ds(pl.multiple_of(g * width, width), width)
        b_at = pl.ds(pl.multiple_of(g * STATE, STATE), STATE)
        c_at = pl.ds(pl.multiple_of((groups + g) * STATE, STATE), STATE)
        b_g = conv(halo_bc[:, b_at], bc_ref[:, b_at], taps_bc[:, b_at])
        bs[g] = b_g
        cs[g] = conv(halo_bc[:, c_at], bc_ref[:, c_at], taps_bc[:, c_at])
        cum = lax.dot(tri, rate_ref[g], precision=lax.Precision.HIGHEST,
                      preferred_element_type=jnp.float32)
        col = jnp.where(is_fwd, cum, -cum)
        row = lw_ref[g] - col
        colt[g] = col
        rowt[g] = row.T
        end = cum[tokens - 1 : tokens]
        to_end = hi_lo(jnp.exp2(row + jnp.where(is_fwd, end, 0.0)))
        lead_hl[g] = hi_lo(jnp.exp2(jnp.where(is_fwd, cum, end - cum)))
        total = hi_lo(jnp.broadcast_to(jnp.exp2(end), (16, 128)))
        x_g = conv(halo_x[:, wide], x_ref[:, wide], taps_x[:, wide])
        xc[g] = x_g
        xf = x_g.astype(jnp.float32)
        across = (((0,), (0,)), ((), ()))
        sent = (xf * dot(to_end, expand[1])).astype(jnp.bfloat16)
        s_send[g] = lax.dot_general(b_g, sent, across, preferred_element_type=jnp.float32).astype(jnp.bfloat16)
        t_send[g] = dot(total, expand[1])[:8]
        s_copy(g).start()
        t_copy(g).start()
        kept = (xf * dot(to_end, expand[0])).astype(jnp.bfloat16)
        s_own[g] = lax.dot_general(b_g, kept, across, preferred_element_type=jnp.float32)
        t_own[g] = dot(total, expand[0])[:8]

    def relay(g):
        s_copy(g).wait_recv()
        t_copy(g).wait_recv()

        @pl.when(has_prev)
        def _():
            chain_copy(g).wait_recv()

        @pl.when(pos == 0)
        def _():
            chain_in[g] = jnp.zeros_like(chain_in[g])

        follow_copy(g).start()
        state = t_in[g][0:1] * chain_in[g].astype(jnp.float32) + s_in[g].astype(jnp.float32)
        h_lead[g] = state.astype(jnp.bfloat16)

        @pl.when(has_next)
        def _():
            chain_out[g] = (t_own[g][0:1] * state + s_own[g]).astype(jnp.bfloat16)
            chain_copy(g).start()

    slots = 2 * groups

    left = lax.broadcasted_iota(jnp.int32, (tokens, 128), 1) < HEADDIM
    lower = rows[:half, :half] >= cols[:half, :half]

    @pl.loop(0, groups)
    def _(g):
        score = lax.dot_general(cs[g], bs[g], (((1,), (1,)), ((), ())), preferred_element_type=jnp.float32)
        for part in range(2):
            turn = 2 * g + part - 2 * pos

            @pl.when((turn >= 0) & (turn < groups))
            def _():
                relay(turn)

            for pair in range(part * PER // 4, (part + 1) * PER // 4):
                at = pair * 2 * HEADDIM
                x_pair = xc[g, :, at : at + 2 * HEADDIM]
                got = []
                for head in (2 * pair, 2 * pair + 1):
                    cf = colt[g, :, head : head + 1]
                    cb = colt[g, :, PER + head : PER + head + 1]
                    rf = rowt[g, head : head + 1, :]
                    rb = rowt[g, PER + head : PER + head + 1, :]
                    tl = jnp.where(lower, cf[:half] + rf[:, :half], cb[:half] + rb[:, :half])
                    tr = cb[:half] + rb[:, half:]
                    bl = cf[half:] + rf[:, :half]
                    br = jnp.where(lower, cf[half:] + rf[:, half:], cb[half:] + rb[:, half:])
                    top = jnp.concatenate([tl, tr], axis=1)
                    bottom = jnp.concatenate([bl, br], axis=1)
                    mix_top = (score[:half] * jnp.exp2(top)).astype(jnp.bfloat16)
                    mix_bottom = (score[half:] * jnp.exp2(bottom)).astype(jnp.bfloat16)
                    got.append(dot(jnp.concatenate([mix_top, mix_bottom], axis=0), x_pair))
                y_acc[g, :, at : at + 2 * HEADDIM] = jnp.where(left, got[0], got[1])

    vis = span_ref.shape[0]
    spans = jnp.concatenate([span_ref[...], span_in[...]], axis=0)
    token = index * tokens + lax.broadcasted_iota(jnp.int32, (2 * vis, tokens), 1)
    inside = ((token >= spans[:, 0:1]) & (token < spans[:, 1:2])).astype(jnp.float32).astype(jnp.bfloat16)
    length = jnp.maximum(spans[:vis, 1:2] - spans[:vis, 0:1], 1).astype(jnp.float32)

    @pl.loop(0, groups)
    def _(g):
        @pl.when(g + 2 * pos >= slots)
        def _():
            relay(g)

        wide = pl.ds(pl.multiple_of(g * width, width), width)
        c_g = cs[g]
        lead = dot(lead_hl[g], expand[0]) * dot(c_g, h_lead[g])
        mixed = y_acc[g] + lead + skip_ref[:, wide] * xc[g].astype(jnp.float32)
        follow_copy(g).wait_recv()
        mixed = mixed + dot(lead_hl[g], expand[1]) * dot(c_g, follow_in[g])
        gated = mixed * silu(gate_ref[:, wide].astype(jnp.float32))
        mean_sq = jnp.mean(gated * gated, axis=1, keepdims=True)
        token_out = (gated * lax.rsqrt(mean_sq + 1e-05) * gain_ref[:, wide]).astype(jnp.bfloat16)
        out_ref[:, wide] = token_out
        sums = dot(inside, token_out)
        own_pool[g] = sums[:vis]
        spill_out[g] = sums[vis:]

        @pl.when(index > 0)
        def _():
            spill_copy(g).start()

    @pl.loop(0, groups)
    def _(g):
        wide = pl.ds(pl.multiple_of(g * width, width), width)

        @pl.when(index < last_index)
        def _():
            spill_copy(g).wait_recv()
            pool_ref[:, wide] = ((own_pool[g] + spill_in[g]) / length).astype(jnp.bfloat16)

        @pl.when(index == last_index)
        def _():
            pool_ref[:, wide] = (own_pool[g] / length).astype(jnp.bfloat16)

    @pl.loop(0, groups)
    def _(g):
        s_copy(g).wait_send()
        t_copy(g).wait_send()
        follow_copy(g).wait_send()

        @pl.when(has_next)
        def _():
            chain_copy(g).wait_send()

        @pl.when(index > 0)
        def _():
            spill_copy(g).wait_send()

    @pl.when(index < last_index)
    def _():
        for copy in halos:
            copy.wait_send()


def on_device(
    x_in, bc_in, gate_z, log_decay, resets, conv_x, conv_bc, skip_d, norm_gain, visit_span
):
    tokens, channels = x_in.shape
    groups = bc_in.shape[2] // STATE
    width = PER * HEADDIM
    vis = visit_span.shape[0]

    def by_group(v):
        v = v.reshape(2, tokens, groups, PER).transpose(2, 1, 0, 3).reshape(groups, tokens, 2 * PER)
        return jnp.pad(v, ((0, 0), (0, 0), (0, 128 - 2 * PER)))

    rate = by_group(log_decay * LOG2E - BIG * resets.astype(jnp.float32)[None, :, None])
    log_weight = by_group(jnp.maximum(0.5 * jnp.log2(-jnp.expm1(2.0 * log_decay)), -1000.0))
    spans = jnp.pad(visit_span, ((0, 0), (0, 126)))
    f32, bf16 = jnp.float32, jnp.bfloat16
    state = (groups, STATE, width)
    whole = pl.BlockSpec(memory_space=pltpu.VMEM)
    pair = pltpu.SemaphoreType.DMA((2, groups))
    return pl.pallas_call(
        functools.partial(kernel, lax.axis_size("ctx"), groups),
        out_shape=(
            jax.ShapeDtypeStruct((tokens, channels), bf16),
            jax.ShapeDtypeStruct((vis, channels), bf16),
        ),
        in_specs=[whole] * 10,
        out_specs=(whole, whole),
        scratch_shapes=[
            pltpu.VMEM((HALO, channels), bf16),
            pltpu.VMEM((HALO, 2 * groups * STATE), bf16),
            pltpu.VMEM((vis, 128), jnp.int32),
            pltpu.VMEM((groups, tokens, width), bf16),
            pltpu.VMEM((groups, tokens, STATE), bf16),
            pltpu.VMEM((groups, tokens, STATE), bf16),
            pltpu.VMEM((groups, tokens, 128), f32),
            pltpu.VMEM((groups, 128, tokens), f32),
            pltpu.VMEM((groups, tokens, 128), bf16),
            pltpu.VMEM((2, 128, width), bf16),
            pltpu.VMEM((groups, tokens, width), f32),
            pltpu.VMEM(state, bf16),
            pltpu.VMEM(state, f32),
            pltpu.VMEM((groups, 8, width), f32),
            pltpu.VMEM(state, bf16),
            pltpu.VMEM((groups, 8, width), f32),
            pltpu.VMEM(state, bf16),
            pltpu.VMEM((groups, 8, width), f32),
            pltpu.VMEM(state, bf16),
            pltpu.VMEM(state, bf16),
            pltpu.VMEM(state, bf16),
            pltpu.VMEM((groups, vis, width), f32),
            pltpu.VMEM((groups, vis, width), f32),
            pltpu.VMEM((groups, vis, width), f32),
            pltpu.SemaphoreType.DMA((2, 3)),
            pair, pair, pair, pair, pair,
        ],
        compiler_params=pltpu.CompilerParams(
            collective_id=0, has_side_effects=True, vmem_limit_bytes=60 << 20
        ),
    )(
        x_in,
        bc_in.reshape(tokens, 2 * groups * STATE),
        gate_z,
        rate,
        log_weight,
        conv_x,
        conv_bc.reshape(4, 2 * groups * STATE),
        jnp.repeat(skip_d, HEADDIM)[None, :],
        norm_gain[None, :],
        spans,
    )


def solution(mesh):
    return jax.shard_map(
        on_device,
        mesh=mesh,
        in_specs=(
            P(("groups", "ctx", "dp"), "tp"),
            P(("groups", "ctx", "dp"), None, "tp"),
            P(("groups", "ctx", "dp"), "tp"),
            P(None, ("groups", "ctx", "dp"), "tp"),
            P(("groups", "ctx", "dp")),
            P(None, "tp"),
            P(None, None, "tp"),
            P("tp"),
            P("tp"),
            P(("groups", "ctx", "dp"), None),
        ),
        out_specs=(P(("groups", "ctx", "dp"), "tp"), P(("groups", "ctx", "dp"), "tp")),
        check_vma=False,
    )
```

```python
import functools
import jax
import jax.numpy as jnp
from jax import lax
from jax.experimental import pallas as pl
from jax.experimental.pallas import tpu as pltpu
from jax.sharding import PartitionSpec as P

HEADDIM = 64
STATE = 128
GROUPS = 8
PER = 16
LOG2E = 1.4426950408889634
BIG = 160.0
LIMIT = 34
HALO = 8
MESH = pl.DeviceIdType.MESH


def silu(v):
    return v / (1.0 + jnp.exp(-v))


def conv(rim, block, taps):
    padded = jnp.concatenate([rim.astype(jnp.float32), block.astype(jnp.float32)], axis=0)
    total = taps[3] * padded[HALO:]
    for k in range(3):
        total = total + taps[k] * pltpu.roll(padded, 3 - k, 0)[HALO:]
    return silu(total).astype(jnp.bfloat16)


def dot(a, b):
    return jnp.dot(a, b, preferred_element_type=jnp.float32)


def kernel(
    chips,
    groups,
    x_ref, bc_ref, gate_ref, rate_ref, reset_ref, taps_x, taps_bc, skip_ref, gain_ref, span_ref,
    out_ref, pool_ref,
    halo_x, halo_bc, span_in, xc, bs, cs, colt, rowt, lead_hl, expand, y_acc, h_lead,
    s_own, t_own, s_send, t_send, s_in, t_in, chain_in, follow_in, chain_out,
    own_pool, spill_out, spill_in,
    sem_halo, sem_s, sem_t, sem_chain, sem_follow, sem_spill,
):
    tokens = x_ref.shape[0]
    width = PER * HEADDIM
    half = tokens // 2
    c = lax.axis_index("ctx")
    d = lax.axis_index("dp")
    other = 1 - d
    nxt = c + 2 * d - 1
    prv = c - 2 * d + 1
    pos = d * c + (1 - d) * (chips - 1 - c)
    has_next = pos < chips - 1
    has_prev = pos > 0
    index = c * 2 + d
    last_index = chips * 2 - 1
    partner = {"ctx": c, "dp": other}
    halo_to = {"ctx": d * nxt + (1 - d) * c, "dp": other}
    spill_to = {"ctx": d * c + (1 - d) * nxt, "dp": other}
    follow_chain = {"ctx": nxt, "dp": d}

    barrier = pltpu.get_barrier_semaphore()
    pl.semaphore_signal(barrier, inc=1, device_id=partner, device_id_type=MESH)

    @pl.when(has_next)
    def _():
        pl.semaphore_signal(barrier, inc=1, device_id={"ctx": nxt, "dp": other}, device_id_type=MESH)
        pl.semaphore_signal(barrier, inc=1, device_id={"ctx": nxt, "dp": d}, device_id_type=MESH)

    @pl.when(has_prev)
    def _():
        pl.semaphore_signal(barrier, inc=1, device_id={"ctx": prv, "dp": d}, device_id_type=MESH)

    pl.semaphore_wait(barrier, 1 + 2 * has_next.astype(jnp.int32) + has_prev.astype(jnp.int32))

    def remote(src, dst, sems, k, to):
        return pltpu.make_async_remote_copy(
            src_ref=src, dst_ref=dst, send_sem=sems.at[0, k], recv_sem=sems.at[1, k],
            device_id=to, device_id_type=MESH,
        )

    tail = pl.ds(tokens - HALO, HALO)
    halos = (
        remote(x_ref.at[tail], halo_x, sem_halo, 0, halo_to),
        remote(bc_ref.at[tail], halo_bc, sem_halo, 1, halo_to),
        remote(span_ref, span_in, sem_halo, 2, halo_to),
    )

    @pl.when(index < last_index)
    def _():
        for copy in halos:
            copy.start()

    def s_copy(g):
        return remote(s_send.at[g], s_in.at[g], sem_s, g, partner)

    def t_copy(g):
        return remote(t_send.at[g], t_in.at[g], sem_t, g, partner)

    def chain_copy(g):
        return remote(chain_out.at[g], chain_in.at[g], sem_chain, g, follow_chain)

    def follow_copy(g):
        return remote(chain_in.at[g], follow_in.at[g], sem_follow, g, partner)

    def spill_copy(g):
        return remote(spill_out.at[g], spill_in.at[g], sem_spill, g, spill_to)

    rows = lax.broadcasted_iota(jnp.int32, (tokens, tokens), 0)
    cols = lax.broadcasted_iota(jnp.int32, (tokens, tokens), 1)
    tri = (rows >= cols).astype(jnp.float32)
    is_fwd = lax.broadcasted_iota(jnp.int32, (2 * PER, tokens), 0) < PER
    erow = lax.rem(lax.broadcasted_iota(jnp.int32, (4 * PER, width), 0), 2 * PER)
    ehead = lax.div(lax.broadcasted_iota(jnp.int32, (4 * PER, width), 1), HEADDIM)
    expand[0] = (erow == ehead + PER * (1 - d)).astype(jnp.float32).astype(jnp.bfloat16)
    expand[1] = (erow == ehead + PER * d).astype(jnp.float32).astype(jnp.bfloat16)
    fold = BIG * reset_ref[...].astype(jnp.float32)

    @pl.when(index == 0)
    def _():
        halo_x[...] = jnp.zeros_like(halo_x)
        halo_bc[...] = jnp.zeros_like(halo_bc)
        span_in[...] = jnp.zeros_like(span_in)

    @pl.when(index > 0)
    def _():
        for copy in halos:
            copy.wait_recv()

    across = (((0,), (0,)), ((), ()))

    def hi_lo(v):
        hi = v.astype(jnp.bfloat16)
        lo = (v - hi.astype(jnp.float32)).astype(jnp.bfloat16)
        return jnp.concatenate([hi, lo], axis=0)

    def spread(v, which):
        return lax.dot_general(v, expand[which], across, preferred_element_type=jnp.float32)

    def spread_end(v, which):
        picked = expand[which, : 2 * PER].astype(jnp.float32) * v
        return jnp.broadcast_to(jnp.sum(picked, axis=0, keepdims=True), (8, width))

    def taps_of(ref, which, at):
        return [ref[k, which : which + 1, at] for k in range(4)]

    @pl.loop(0, groups)
    def _(g):
        wide = pl.ds(pl.multiple_of(g * width, width), width)
        b_at = pl.ds(pl.multiple_of(g * STATE, STATE), STATE)
        c_at = pl.ds(pl.multiple_of((groups + g) * STATE, STATE), STATE)
        b_g = conv(halo_bc[:, b_at], bc_ref[:, b_at], taps_of(taps_bc, 0, b_at))
        bs[g] = b_g
        cs[g] = conv(halo_bc[:, c_at], bc_ref[:, c_at], taps_of(taps_bc, 1, b_at))
        heads = pl.ds(pl.multiple_of(g * PER, PER), PER)
        rate = jnp.concatenate([rate_ref[0, heads, :], rate_ref[1, heads, :]], axis=0)
        cum = lax.dot_general(rate * LOG2E - fold, tri, (((1,), (1,)), ((), ())),
                              precision=lax.Precision.HIGHEST, preferred_element_type=jnp.float32)
        r = -2.0 * rate
        small = r * (1.0 - r * (1 / 2 - r * (1 / 6 - r * (1 / 24 - r * (1 / 120 - r / 720)))))
        loss = jnp.where(r < 0.25, small, 1.0 - jnp.exp(-r))
        log_weight = jnp.maximum((0.5 * LOG2E) * jnp.log(loss), -1000.0)
        col = jnp.where(is_fwd, cum, -cum)
        row = log_weight - col
        colt[g] = col.T
        rowt[g] = row
        end = cum[:, tokens - 1 : tokens]
        to_end = hi_lo(jnp.exp2(row + jnp.where(is_fwd, end, 0.0)))
        lead_hl[g] = hi_lo(jnp.exp2(jnp.where(is_fwd, cum, end - cum)))
        total = jnp.exp2(end)
        x_g = conv(halo_x[:, wide], x_ref[:, wide], [taps_x[k : k + 1, wide] for k in range(4)])
        xc[g] = x_g
        xf = x_g.astype(jnp.float32)
        sent = (xf * spread(to_end, 1)).astype(jnp.bfloat16)
        s_send[g] = lax.dot_general(b_g, sent, across, preferred_element_type=jnp.float32).astype(jnp.bfloat16)
        t_send[g] = spread_end(total, 1)
        s_copy(g).start()
        t_copy(g).start()
        kept = (xf * spread(to_end, 0)).astype(jnp.bfloat16)
        s_own[g] = lax.dot_general(b_g, kept, across, preferred_element_type=jnp.float32)
        t_own[g] = spread_end(total, 0)

    def relay(g):
        s_copy(g).wait_recv()
        t_copy(g).wait_recv()

        @pl.when(has_prev)
        def _():
            chain_copy(g).wait_recv()

        @pl.when(pos == 0)
        def _():
            chain_in[g] = jnp.zeros_like(chain_in[g])

        follow_copy(g).start()
        state = t_in[g][0:1] * chain_in[g].astype(jnp.float32) + s_in[g].astype(jnp.float32)
        h_lead[g] = state.astype(jnp.bfloat16)

        @pl.when(has_next)
        def _():
            chain_out[g] = (t_own[g][0:1] * state + s_own[g]).astype(jnp.bfloat16)
            chain_copy(g).start()

    slots = 2 * groups

    left = lax.broadcasted_iota(jnp.int32, (tokens, 128), 1) < HEADDIM
    lower = rows[:half, :half] >= cols[:half, :half]

    @pl.loop(0, groups)
    def _(g):
        score = lax.dot_general(cs[g], bs[g], (((1,), (1,)), ((), ())), preferred_element_type=jnp.float32)
        for part in range(2):
            turn = 2 * g + part - 2 * pos

            @pl.when((turn >= 0) & (turn < groups))
            def _():
                relay(turn)

            for pair in range(part * PER // 4, (part + 1) * PER // 4):
                at = pair * 2 * HEADDIM
                x_pair = xc[g, :, at : at + 2 * HEADDIM]
                got = []
                for head in (2 * pair, 2 * pair + 1):
                    cf = colt[g, :, head : head + 1]
                    cb = colt[g, :, PER + head : PER + head + 1]
                    rf = rowt[g, head : head + 1, :]
                    rb = rowt[g, PER + head : PER + head + 1, :]
                    tl = jnp.where(lower, cf[:half] + rf[:, :half], cb[:half] + rb[:, :half])
                    tr = cb[:half] + rb[:, half:]
                    bl = cf[half:] + rf[:, :half]
                    br = jnp.where(lower, cf[half:] + rf[:, half:], cb[half:] + rb[:, half:])
                    top = jnp.concatenate([tl, tr], axis=1)
                    bottom = jnp.concatenate([bl, br], axis=1)
                    mix_top = (score[:half] * jnp.exp2(top)).astype(jnp.bfloat16)
                    mix_bottom = (score[half:] * jnp.exp2(bottom)).astype(jnp.bfloat16)
                    got.append(dot(jnp.concatenate([mix_top, mix_bottom], axis=0), x_pair))
                y_acc[g, :, at : at + 2 * HEADDIM] = jnp.where(left, got[0], got[1])

    vis = span_ref.shape[1]
    token = index * tokens + lax.broadcasted_iota(jnp.int32, (tokens, vis), 0)

    def covers(ref):
        return ((token >= ref[0:1]) & (token < ref[1:2])).astype(jnp.float32).T

    inside = jnp.concatenate([covers(span_ref), covers(span_in)], axis=0).astype(jnp.bfloat16)
    same = lax.broadcasted_iota(jnp.int32, (vis, vis), 0) == lax.broadcasted_iota(jnp.int32, (vis, vis), 1)
    spanned = jnp.maximum(span_ref[1:2] - span_ref[0:1], 1).astype(jnp.float32)
    length = jnp.sum(jnp.where(same, spanned, 0.0), axis=1, keepdims=True)

    def skip_of(g):
        at = lax.broadcasted_iota(jnp.int32, (groups * PER, width), 0)
        head = lax.div(lax.broadcasted_iota(jnp.int32, (groups * PER, width), 1), HEADDIM)
        pick = (at == head + g * PER).astype(jnp.float32)
        skips = jnp.broadcast_to(skip_ref[...], (8, groups * PER))
        return lax.dot(skips, pick, precision=lax.Precision.HIGHEST,
                       preferred_element_type=jnp.float32)[0:1]

    @pl.loop(0, groups)
    def _(g):
        @pl.when(g + 2 * pos >= slots)
        def _():
            relay(g)

        wide = pl.ds(pl.multiple_of(g * width, width), width)
        c_g = cs[g]
        lead = spread(lead_hl[g], 0) * dot(c_g, h_lead[g])
        mixed = y_acc[g] + lead + skip_of(g) * xc[g].astype(jnp.float32)
        follow_copy(g).wait_recv()
        mixed = mixed + spread(lead_hl[g], 1) * dot(c_g, follow_in[g])
        gated = mixed * silu(gate_ref[:, wide].astype(jnp.float32))
        mean_sq = jnp.mean(gated * gated, axis=1, keepdims=True)
        token_out = (gated * lax.rsqrt(mean_sq + 1e-05) * gain_ref[:, wide]).astype(jnp.bfloat16)
        out_ref[:, wide] = token_out
        sums = dot(inside, token_out)
        own_pool[g] = sums[:vis]
        spill_out[g] = sums[vis:]

        @pl.when(index > 0)
        def _():
            spill_copy(g).start()

    @pl.loop(0, groups)
    def _(g):
        wide = pl.ds(pl.multiple_of(g * width, width), width)

        @pl.when(index < last_index)
        def _():
            spill_copy(g).wait_recv()
            pool_ref[:, wide] = ((own_pool[g] + spill_in[g]) / length).astype(jnp.bfloat16)

        @pl.when(index == last_index)
        def _():
            pool_ref[:, wide] = (own_pool[g] / length).astype(jnp.bfloat16)

    @pl.loop(0, groups)
    def _(g):
        s_copy(g).wait_send()
        t_copy(g).wait_send()
        follow_copy(g).wait_send()

        @pl.when(has_next)
        def _():
            chain_copy(g).wait_send()

        @pl.when(index > 0)
        def _():
            spill_copy(g).wait_send()

    @pl.when(index < last_index)
    def _():
        for copy in halos:
            copy.wait_send()


def on_device(
    x_in, bc_in, gate_z, log_decay, resets, conv_x, conv_bc, skip_d, norm_gain, visit_span
):
    tokens, channels = x_in.shape
    groups = bc_in.shape[2] // STATE
    width = PER * HEADDIM
    vis = visit_span.shape[0]

    f32, bf16 = jnp.float32, jnp.bfloat16
    state = (groups, STATE, width)
    whole = pl.BlockSpec(memory_space=pltpu.VMEM)
    pair = pltpu.SemaphoreType.DMA((2, groups))
    return pl.pallas_call(
        functools.partial(kernel, lax.axis_size("ctx"), groups),
        out_shape=(
            jax.ShapeDtypeStruct((tokens, channels), bf16),
            jax.ShapeDtypeStruct((vis, channels), bf16),
        ),
        in_specs=[whole] * 10,
        out_specs=(whole, whole),
        scratch_shapes=[
            pltpu.VMEM((HALO, channels), bf16),
            pltpu.VMEM((HALO, 2 * groups * STATE), bf16),
            pltpu.VMEM((2, vis), jnp.int32),
            pltpu.VMEM((groups, tokens, width), bf16),
            pltpu.VMEM((groups, tokens, STATE), bf16),
            pltpu.VMEM((groups, tokens, STATE), bf16),
            pltpu.VMEM((groups, tokens, 2 * PER), f32),
            pltpu.VMEM((groups, 2 * PER, tokens), f32),
            pltpu.VMEM((groups, 4 * PER, tokens), bf16),
            pltpu.VMEM((2, 4 * PER, width), bf16),
            pltpu.VMEM((groups, tokens, width), f32),
            pltpu.VMEM(state, bf16),
            pltpu.VMEM(state, f32),
            pltpu.VMEM((groups, 8, width), f32),
            pltpu.VMEM(state, bf16),
            pltpu.VMEM((groups, 8, width), f32),
            pltpu.VMEM(state, bf16),
            pltpu.VMEM((groups, 8, width), f32),
            pltpu.VMEM(state, bf16),
            pltpu.VMEM(state, bf16),
            pltpu.VMEM(state, bf16),
            pltpu.VMEM((groups, vis, width), f32),
            pltpu.VMEM((groups, vis, width), f32),
            pltpu.VMEM((groups, vis, width), f32),
            pltpu.SemaphoreType.DMA((2, 3)),
            pair, pair, pair, pair, pair,
        ],
        compiler_params=pltpu.CompilerParams(
            collective_id=0, has_side_effects=True, vmem_limit_bytes=LIMIT << 20
        ),
    )(
        x_in,
        bc_in.reshape(tokens, 2 * groups * STATE),
        gate_z,
        log_decay.transpose(0, 2, 1),
        resets[None, :],
        conv_x,
        conv_bc,
        skip_d[None, :],
        norm_gain[None, :],
        visit_span.T,
    )


def solution(mesh):
    return jax.shard_map(
        on_device,
        mesh=mesh,
        in_specs=(
            P(("groups", "ctx", "dp"), "tp"),
            P(("groups", "ctx", "dp"), None, "tp"),
            P(("groups", "ctx", "dp"), "tp"),
            P(None, ("groups", "ctx", "dp"), "tp"),
            P(("groups", "ctx", "dp")),
            P(None, "tp"),
            P(None, None, "tp"),
            P("tp"),
            P("tp"),
            P(("groups", "ctx", "dp"), None),
        ),
        out_specs=(P(("groups", "ctx", "dp"), "tp"), P(("groups", "ctx", "dp"), "tp")),
        check_vma=False,
    )
```

```python
import functools
import jax
import jax.numpy as jnp
from jax import lax
from jax.experimental import pallas as pl
from jax.experimental.pallas import tpu as pltpu
from jax.sharding import PartitionSpec as P

HEADDIM = 64
STATE = 128
GROUPS = 8
PER = 16
LOG2E = 1.4426950408889634
BIG = 160.0
LIMIT = 57
HALO = 8
MESH = pl.DeviceIdType.MESH


def silu(v):
    return v / (1.0 + jnp.exp(-v))


def conv(rim, block, taps):
    padded = jnp.concatenate([rim.astype(jnp.float32), block.astype(jnp.float32)], axis=0)
    total = taps[3] * padded[HALO:]
    for k in range(3):
        total = total + taps[k] * pltpu.roll(padded, 3 - k, 0)[HALO:]
    return silu(total).astype(jnp.bfloat16)


def dot(a, b):
    return jnp.dot(a, b, preferred_element_type=jnp.float32)


def kernel(
    chips,
    groups,
    x_hbm, bc_hbm, gate_hbm, rate_hbm, reset_hbm, taps_x_hbm, taps_bc_hbm, skip_hbm, gain_hbm, span_hbm,
    out_ref, pool_ref,
    x_ref, bc_ref, gate_ref, rate_ref, reset_ref, taps_x, taps_bc, skip_ref, gain_ref, span_ref,
    halo_x, halo_bc, span_in, xc, bs, cs, colt, rowt, lead_hl, expand, y_acc, h_lead,
    s_own, t_own, s_send, t_send, s_in, t_in, chain_in, follow_in, chain_out,
    own_pool, spill_out, spill_in,
    sem_in, sem_halo, sem_s, sem_t, sem_chain, sem_follow, sem_spill,
):
    tokens = x_ref.shape[0]
    width = PER * HEADDIM
    half = tokens // 2
    part = width // 2
    chunks = 2 * groups
    c = lax.axis_index("ctx")
    d = lax.axis_index("dp")
    other = 1 - d
    nxt = c + 2 * d - 1
    prv = c - 2 * d + 1
    pos = d * c + (1 - d) * (chips - 1 - c)
    has_next = pos < chips - 1
    has_prev = pos > 0
    index = c * 2 + d
    last_index = chips * 2 - 1
    partner = {"ctx": c, "dp": other}
    halo_to = {"ctx": d * nxt + (1 - d) * c, "dp": other}
    spill_to = {"ctx": d * c + (1 - d) * nxt, "dp": other}
    follow_chain = {"ctx": nxt, "dp": d}

    sources = (x_hbm, bc_hbm, rate_hbm, reset_hbm, taps_x_hbm, taps_bc_hbm, gate_hbm, skip_hbm, gain_hbm, span_hbm)
    places = (x_ref, bc_ref, rate_ref, reset_ref, taps_x, taps_bc, gate_ref, skip_ref, gain_ref, span_ref)
    loads = [pltpu.make_async_copy(sources[k], places[k], sem_in.at[k]) for k in range(10)]
    for load in loads:
        load.start()

    barrier = pltpu.get_barrier_semaphore()
    pl.semaphore_signal(barrier, inc=1, device_id=partner, device_id_type=MESH)

    @pl.when(has_next)
    def _():
        pl.semaphore_signal(barrier, inc=1, device_id={"ctx": nxt, "dp": other}, device_id_type=MESH)
        pl.semaphore_signal(barrier, inc=1, device_id={"ctx": nxt, "dp": d}, device_id_type=MESH)

    @pl.when(has_prev)
    def _():
        pl.semaphore_signal(barrier, inc=1, device_id={"ctx": prv, "dp": d}, device_id_type=MESH)

    pl.semaphore_wait(barrier, 1 + 2 * has_next.astype(jnp.int32) + has_prev.astype(jnp.int32))

    def remote(src, dst, sems, k, to):
        return pltpu.make_async_remote_copy(
            src_ref=src, dst_ref=dst, send_sem=sems.at[0, k], recv_sem=sems.at[1, k],
            device_id=to, device_id_type=MESH,
        )

    tail = pl.ds(tokens - HALO, HALO)
    halos = (
        remote(x_hbm.at[tail], halo_x, sem_halo, 0, halo_to),
        remote(bc_hbm.at[tail], halo_bc, sem_halo, 1, halo_to),
        remote(span_hbm, span_in, sem_halo, 2, halo_to),
    )

    @pl.when(index < last_index)
    def _():
        for copy in halos:
            copy.start()

    def s_copy(g):
        return remote(s_send.at[g], s_in.at[g], sem_s, g, partner)

    def t_copy(g):
        return remote(t_send.at[g], t_in.at[g], sem_t, g, partner)

    def chain_copy(g):
        return remote(chain_out.at[g], chain_in.at[g], sem_chain, g, follow_chain)

    def follow_copy(g):
        return remote(chain_in.at[g], follow_in.at[g], sem_follow, g, partner)

    def spill_copy(g):
        return remote(spill_out.at[g], spill_in.at[g], sem_spill, g, spill_to)

    rows = lax.broadcasted_iota(jnp.int32, (tokens, tokens), 0)
    cols = lax.broadcasted_iota(jnp.int32, (tokens, tokens), 1)
    tri = (rows >= cols).astype(jnp.float32)
    is_fwd = lax.broadcasted_iota(jnp.int32, (2 * PER, tokens), 0) < PER
    erow = lax.rem(lax.broadcasted_iota(jnp.int32, (4 * PER, width), 0), 2 * PER)
    ehead = lax.div(lax.broadcasted_iota(jnp.int32, (4 * PER, width), 1), HEADDIM)
    expand[0] = (erow == ehead + PER * (1 - d)).astype(jnp.float32).astype(jnp.bfloat16)
    expand[1] = (erow == ehead + PER * d).astype(jnp.float32).astype(jnp.bfloat16)
    for load in loads[:6]:
        load.wait()

    fold = BIG * reset_ref[...].astype(jnp.float32)

    @pl.when(index == 0)
    def _():
        halo_x[...] = jnp.zeros_like(halo_x)
        halo_bc[...] = jnp.zeros_like(halo_bc)
        span_in[...] = jnp.zeros_like(span_in)

    @pl.when(index > 0)
    def _():
        for copy in halos:
            copy.wait_recv()

    across = (((0,), (0,)), ((), ()))

    def hi_lo(v):
        hi = v.astype(jnp.bfloat16)
        lo = (v - hi.astype(jnp.float32)).astype(jnp.bfloat16)
        return jnp.concatenate([hi, lo], axis=0)

    def spread(v, which):
        return lax.dot_general(v, expand[which], across, preferred_element_type=jnp.float32)

    def spread_end(v, which):
        picked = expand[which, : 2 * PER].astype(jnp.float32) * v
        return jnp.broadcast_to(jnp.sum(picked, axis=0, keepdims=True), (8, width))

    def taps_of(ref, which, at):
        return [ref[k, which : which + 1, at] for k in range(4)]

    def relay(g):
        s_copy(g).wait_recv()
        t_copy(g).wait_recv()

        @pl.when(has_prev)
        def _():
            chain_copy(g).wait_recv()

        @pl.when(pos == 0)
        def _():
            chain_in[g] = jnp.zeros_like(chain_in[g])

        follow_copy(g).start()
        state = t_in[g][0:1] * chain_in[g].astype(jnp.float32) + s_in[g].astype(jnp.float32)
        h_lead[g] = state.astype(jnp.bfloat16)

        @pl.when(has_next)
        def _():
            chain_out[g] = (t_own[g][0:1] * state + s_own[g]).astype(jnp.bfloat16)
            chain_copy(g).start()

    @pl.loop(0, groups)
    def _(g):
        wide = pl.ds(pl.multiple_of(g * width, width), width)
        b_at = pl.ds(pl.multiple_of(g * STATE, STATE), STATE)
        c_at = pl.ds(pl.multiple_of((groups + g) * STATE, STATE), STATE)
        b_g = conv(halo_bc[:, b_at], bc_ref[:, b_at], taps_of(taps_bc, 0, b_at))
        bs[g] = b_g
        cs[g] = conv(halo_bc[:, c_at], bc_ref[:, c_at], taps_of(taps_bc, 1, b_at))
        heads = pl.ds(pl.multiple_of(g * PER, PER), PER)
        rate = jnp.concatenate([rate_ref[0, heads, :], rate_ref[1, heads, :]], axis=0)
        cum = lax.dot_general(rate * LOG2E - fold, tri, (((1,), (1,)), ((), ())),
                              precision=lax.Precision.HIGHEST, preferred_element_type=jnp.float32)
        r = -2.0 * rate
        small = r * (1.0 - r * (1 / 2 - r * (1 / 6 - r * (1 / 24 - r * (1 / 120 - r / 720)))))
        loss = jnp.where(r < 0.25, small, 1.0 - jnp.exp(-r))
        log_weight = jnp.maximum((0.5 * LOG2E) * jnp.log(loss), -1000.0)
        col = jnp.where(is_fwd, cum, -cum)
        row = log_weight - col
        colt[g] = col.T
        rowt[g] = row
        end = cum[:, tokens - 1 : tokens]
        to_end = hi_lo(jnp.exp2(row + jnp.where(is_fwd, end, 0.0)))
        lead_hl[g] = hi_lo(jnp.exp2(jnp.where(is_fwd, cum, end - cum)))
        total = jnp.exp2(end)
        x_g = conv(halo_x[:, wide], x_ref[:, wide], [taps_x[k : k + 1, wide] for k in range(4)])
        xc[g] = x_g
        xf = x_g.astype(jnp.float32)
        sent = (xf * spread(to_end, 1)).astype(jnp.bfloat16)
        state = lax.dot_general(b_g, sent, across, preferred_element_type=jnp.float32)
        ends = spread_end(total, 1)
        for k in range(2):
            s_send[2 * g + k] = state[:, k * part : (k + 1) * part].astype(jnp.bfloat16)
            t_send[2 * g + k] = ends[:, k * part : (k + 1) * part]
            s_copy(2 * g + k).start()
            t_copy(2 * g + k).start()
        kept = (xf * spread(to_end, 0)).astype(jnp.bfloat16)
        state = lax.dot_general(b_g, kept, across, preferred_element_type=jnp.float32)
        ends = spread_end(total, 0)
        for k in range(2):
            s_own[2 * g + k] = state[:, k * part : (k + 1) * part]
            t_own[2 * g + k] = ends[:, k * part : (k + 1) * part]

        @pl.when((pos == 0) & (g > 0))
        def _():
            relay(2 * g - 2)
            relay(2 * g - 1)

    slots = 4 * groups
    first = 7 * jnp.maximum(pos - 1, 0) - 4
    done_early = jnp.where(pos == 0, chunks - 2, jnp.where(pos == 1, 2, 0))
    done_before = jnp.where(pos == 0, chunks, jnp.clip(lax.div(slots - first + 2, 3), 0, chunks))

    @pl.when(pos == 0)
    def _():
        relay(chunks - 2)
        relay(chunks - 1)

    @pl.when(pos == 1)
    def _():
        relay(0)
        relay(1)

    left = lax.broadcasted_iota(jnp.int32, (tokens, 128), 1) < HEADDIM
    lower = rows[:half, :half] >= cols[:half, :half]

    @pl.loop(0, groups)
    def _(g):
        score = lax.dot_general(cs[g], bs[g], (((1,), (1,)), ((), ())), preferred_element_type=jnp.float32)
        for quarter in range(4):
            turn = 4 * g + quarter - first

            @pl.when((pos > 0) & (turn >= 0) & (lax.rem(turn, 3) == 0) & (lax.div(turn, 3) >= done_early) & (lax.div(turn, 3) < chunks))
            def _():
                relay(lax.div(turn, 3))

            for pair in range(quarter * PER // 8, (quarter + 1) * PER // 8):
                at = pair * 2 * HEADDIM
                x_pair = xc[g, :, at : at + 2 * HEADDIM]
                got = []
                for head in (2 * pair, 2 * pair + 1):
                    cf = colt[g, :, head : head + 1]
                    cb = colt[g, :, PER + head : PER + head + 1]
                    rf = rowt[g, head : head + 1, :]
                    rb = rowt[g, PER + head : PER + head + 1, :]
                    tl = jnp.where(lower, cf[:half] + rf[:, :half], cb[:half] + rb[:, :half])
                    tr = cb[:half] + rb[:, half:]
                    bl = cf[half:] + rf[:, :half]
                    br = jnp.where(lower, cf[half:] + rf[:, half:], cb[half:] + rb[:, half:])
                    top = jnp.concatenate([tl, tr], axis=1)
                    bottom = jnp.concatenate([bl, br], axis=1)
                    mix_top = (score[:half] * jnp.exp2(top)).astype(jnp.bfloat16)
                    mix_bottom = (score[half:] * jnp.exp2(bottom)).astype(jnp.bfloat16)
                    got.append(dot(jnp.concatenate([mix_top, mix_bottom], axis=0), x_pair))
                y_acc[g, :, at : at + 2 * HEADDIM] = jnp.where(left, got[0], got[1])

    for load in loads[6:]:
        load.wait()

    vis = span_ref.shape[1]
    token = index * tokens + lax.broadcasted_iota(jnp.int32, (tokens, vis), 0)

    def covers(ref):
        return ((token >= ref[0:1]) & (token < ref[1:2])).astype(jnp.float32).T

    inside = jnp.concatenate([covers(span_ref), covers(span_in)], axis=0).astype(jnp.bfloat16)
    same = lax.broadcasted_iota(jnp.int32, (vis, vis), 0) == lax.broadcasted_iota(jnp.int32, (vis, vis), 1)
    spanned = jnp.maximum(span_ref[1:2] - span_ref[0:1], 1).astype(jnp.float32)
    length = jnp.sum(jnp.where(same, spanned, 0.0), axis=1, keepdims=True)

    def skip_of(g):
        at = lax.broadcasted_iota(jnp.int32, (groups * PER, width), 0)
        head = lax.div(lax.broadcasted_iota(jnp.int32, (groups * PER, width), 1), HEADDIM)
        pick = (at == head + g * PER).astype(jnp.float32)
        skips = jnp.broadcast_to(skip_ref[...], (8, groups * PER))
        return lax.dot(skips, pick, precision=lax.Precision.HIGHEST,
                       preferred_element_type=jnp.float32)[0:1]

    @pl.loop(0, groups)
    def _(g):
        begin = jnp.where(g == 0, done_before, jnp.clip(jnp.maximum(2 * g, done_before + 2 * g), 0, chunks))
        finish = jnp.clip(done_before + 2 * g + 2, 0, chunks)

        @pl.when(begin < finish)
        def _():
            relay(begin)

        @pl.when(begin + 1 < finish)
        def _():
            relay(begin + 1)

        wide = pl.ds(pl.multiple_of(g * width, width), width)
        c_g = cs[g]
        lead = spread(lead_hl[g], 0) * dot(c_g, jnp.concatenate([h_lead[2 * g], h_lead[2 * g + 1]], axis=1))
        mixed = y_acc[g] + lead + skip_of(g) * xc[g].astype(jnp.float32)
        follow_copy(2 * g).wait_recv()
        follow_copy(2 * g + 1).wait_recv()
        mixed = mixed + spread(lead_hl[g], 1) * dot(c_g, jnp.concatenate([follow_in[2 * g], follow_in[2 * g + 1]], axis=1))
        gated = mixed * silu(gate_ref[:, wide].astype(jnp.float32))
        mean_sq = jnp.mean(gated * gated, axis=1, keepdims=True)
        token_out = (gated * lax.rsqrt(mean_sq + 1e-05) * gain_ref[:, wide]).astype(jnp.bfloat16)
        out_ref[:, wide] = token_out
        sums = dot(inside, token_out)
        own_pool[g] = sums[:vis]
        spill_out[g] = sums[vis:]

        @pl.when(index > 0)
        def _():
            spill_copy(g).start()

    @pl.loop(0, groups)
    def _(g):
        wide = pl.ds(pl.multiple_of(g * width, width), width)

        @pl.when(index < last_index)
        def _():
            spill_copy(g).wait_recv()
            pool_ref[:, wide] = ((own_pool[g] + spill_in[g]) / length).astype(jnp.bfloat16)

        @pl.when(index == last_index)
        def _():
            pool_ref[:, wide] = (own_pool[g] / length).astype(jnp.bfloat16)

    @pl.loop(0, chunks)
    def _(q):
        s_copy(q).wait_send()
        t_copy(q).wait_send()
        follow_copy(q).wait_send()

        @pl.when(has_next)
        def _():
            chain_copy(q).wait_send()

    @pl.when(index > 0)
    def _():
        @pl.loop(0, groups)
        def _(g):
            spill_copy(g).wait_send()

    @pl.when(index < last_index)
    def _():
        for copy in halos:
            copy.wait_send()


def on_device(
    x_in, bc_in, gate_z, log_decay, resets, conv_x, conv_bc, skip_d, norm_gain, visit_span
):
    tokens, channels = x_in.shape
    groups = bc_in.shape[2] // STATE
    width = PER * HEADDIM
    vis = visit_span.shape[0]

    f32, bf16 = jnp.float32, jnp.bfloat16
    state = (2 * groups, STATE, width // 2)
    ends = (2 * groups, 8, width // 2)
    whole = pl.BlockSpec(memory_space=pltpu.VMEM)
    outside = pl.BlockSpec(memory_space=pltpu.HBM)
    per_chunk = pltpu.SemaphoreType.DMA((2, 2 * groups))
    operands = (
        x_in,
        bc_in.reshape(tokens, 2 * groups * STATE),
        gate_z,
        log_decay.transpose(0, 2, 1),
        resets[None, :],
        conv_x,
        conv_bc,
        skip_d[None, :],
        norm_gain[None, :],
        visit_span.T,
    )
    return pl.pallas_call(
        functools.partial(kernel, lax.axis_size("ctx"), groups),
        out_shape=(
            jax.ShapeDtypeStruct((tokens, channels), bf16),
            jax.ShapeDtypeStruct((vis, channels), bf16),
        ),
        in_specs=[outside] * 10,
        out_specs=(whole, whole),
        scratch_shapes=[
            *(pltpu.VMEM(v.shape, v.dtype) for v in operands),
            pltpu.VMEM((HALO, channels), bf16),
            pltpu.VMEM((HALO, 2 * groups * STATE), bf16),
            pltpu.VMEM((2, vis), jnp.int32),
            pltpu.VMEM((groups, tokens, width), bf16),
            pltpu.VMEM((groups, tokens, STATE), bf16),
            pltpu.VMEM((groups, tokens, STATE), bf16),
            pltpu.VMEM((groups, tokens, 2 * PER), f32),
            pltpu.VMEM((groups, 2 * PER, tokens), f32),
            pltpu.VMEM((groups, 4 * PER, tokens), bf16),
            pltpu.VMEM((2, 4 * PER, width), bf16),
            pltpu.VMEM((groups, tokens, width), f32),
            pltpu.VMEM(state, bf16),
            pltpu.VMEM(state, f32),
            pltpu.VMEM(ends, f32),
            pltpu.VMEM(state, bf16),
            pltpu.VMEM(ends, f32),
            pltpu.VMEM(state, bf16),
            pltpu.VMEM(ends, f32),
            pltpu.VMEM(state, bf16),
            pltpu.VMEM(state, bf16),
            pltpu.VMEM(state, bf16),
            pltpu.VMEM((groups, vis, width), f32),
            pltpu.VMEM((groups, vis, width), f32),
            pltpu.VMEM((groups, vis, width), f32),
            pltpu.SemaphoreType.DMA((10,)),
            pltpu.SemaphoreType.DMA((2, 3)),
            per_chunk, per_chunk, per_chunk, per_chunk,
            pltpu.SemaphoreType.DMA((2, groups)),
        ],
        compiler_params=pltpu.CompilerParams(
            collective_id=0, has_side_effects=True, vmem_limit_bytes=LIMIT << 20
        ),
    )(*operands)


def solution(mesh):
    return jax.shard_map(
        on_device,
        mesh=mesh,
        in_specs=(
            P(("groups", "ctx", "dp"), "tp"),
            P(("groups", "ctx", "dp"), None, "tp"),
            P(("groups", "ctx", "dp"), "tp"),
            P(None, ("groups", "ctx", "dp"), "tp"),
            P(("groups", "ctx", "dp")),
            P(None, "tp"),
            P(None, None, "tp"),
            P("tp"),
            P("tp"),
            P(("groups", "ctx", "dp"), None),
        ),
        out_specs=(P(("groups", "ctx", "dp"), "tp"), P(("groups", "ctx", "dp"), "tp")),
        check_vma=False,
    )
```

```python
import functools
import jax
import jax.numpy as jnp
from jax import lax
from jax.experimental import pallas as pl
from jax.experimental.pallas import tpu as pltpu
from jax.sharding import PartitionSpec as P

HEADDIM = 64
STATE = 128
GROUPS = 8
PER = 16
LOG2E = 1.4426950408889634
BIG = 160.0
LIMIT = 57
HALO = 8
MESH = pl.DeviceIdType.MESH


def silu(v):
    return v / (1.0 + jnp.exp(-v))


def conv(rim, block, taps):
    padded = jnp.concatenate([rim.astype(jnp.float32), block.astype(jnp.float32)], axis=0)
    total = taps[3] * padded[HALO:]
    for k in range(3):
        total = total + taps[k] * pltpu.roll(padded, 3 - k, 0)[HALO:]
    return silu(total).astype(jnp.bfloat16)


def dot(a, b):
    return jnp.dot(a, b, preferred_element_type=jnp.float32)


def kernel(
    chips,
    groups,
    x_hbm, bc_hbm, gate_hbm, rate_hbm, reset_hbm, taps_x_hbm, taps_bc_hbm, skip_hbm, gain_hbm, span_hbm,
    out_hbm, pool_ref,
    out_ref,
    x_ref, bc_ref, gate_ref, rate_ref, reset_ref, taps_x, taps_bc, skip_ref, gain_ref, span_ref,
    halo_x, halo_bc, span_in, xc, bs, cs, colt, rowt, lead_hl, expand, y_acc, h_lead,
    s_own, t_own, s_send, t_send, s_in, t_in, chain_in, follow_in, chain_out,
    own_pool, spill_out, spill_in,
    sem_in, sem_out, sem_halo, sem_s, sem_t, sem_chain, sem_follow, sem_spill,
):
    tokens = x_ref.shape[0]
    width = PER * HEADDIM
    half = tokens // 2
    part = width // 2
    chunks = 2 * groups
    c = lax.axis_index("ctx")
    d = lax.axis_index("dp")
    other = 1 - d
    nxt = c + 2 * d - 1
    prv = c - 2 * d + 1
    pos = d * c + (1 - d) * (chips - 1 - c)
    has_next = pos < chips - 1
    has_prev = pos > 0
    index = c * 2 + d
    last_index = chips * 2 - 1
    partner = {"ctx": c, "dp": other}
    halo_to = {"ctx": d * nxt + (1 - d) * c, "dp": other}
    spill_to = {"ctx": d * c + (1 - d) * nxt, "dp": other}
    follow_chain = {"ctx": nxt, "dp": d}

    sources = (x_hbm, bc_hbm, rate_hbm, reset_hbm, taps_x_hbm, taps_bc_hbm, gate_hbm, skip_hbm, gain_hbm, span_hbm)
    places = (x_ref, bc_ref, rate_ref, reset_ref, taps_x, taps_bc, gate_ref, skip_ref, gain_ref, span_ref)
    loads = [pltpu.make_async_copy(sources[k], places[k], sem_in.at[k]) for k in range(10)]
    for load in loads:
        load.start()

    barrier = pltpu.get_barrier_semaphore()
    pl.semaphore_signal(barrier, inc=1, device_id=partner, device_id_type=MESH)

    @pl.when(has_next)
    def _():
        pl.semaphore_signal(barrier, inc=1, device_id={"ctx": nxt, "dp": other}, device_id_type=MESH)
        pl.semaphore_signal(barrier, inc=1, device_id={"ctx": nxt, "dp": d}, device_id_type=MESH)

    @pl.when(has_prev)
    def _():
        pl.semaphore_signal(barrier, inc=1, device_id={"ctx": prv, "dp": d}, device_id_type=MESH)

    pl.semaphore_wait(barrier, 1 + 2 * has_next.astype(jnp.int32) + has_prev.astype(jnp.int32))

    def remote(src, dst, sems, k, to):
        return pltpu.make_async_remote_copy(
            src_ref=src, dst_ref=dst, send_sem=sems.at[0, k], recv_sem=sems.at[1, k],
            device_id=to, device_id_type=MESH,
        )

    tail = pl.ds(tokens - HALO, HALO)
    halos = (
        remote(x_hbm.at[tail], halo_x, sem_halo, 0, halo_to),
        remote(bc_hbm.at[tail], halo_bc, sem_halo, 1, halo_to),
        remote(span_hbm, span_in, sem_halo, 2, halo_to),
    )

    @pl.when(index < last_index)
    def _():
        for copy in halos:
            copy.start()

    def s_copy(g):
        return remote(s_send.at[g], s_in.at[g], sem_s, g, partner)

    def t_copy(g):
        return remote(t_send.at[g], t_in.at[g], sem_t, g, partner)

    def chain_copy(g):
        return remote(chain_out.at[g], chain_in.at[g], sem_chain, g, follow_chain)

    def follow_copy(g):
        return remote(chain_in.at[g], follow_in.at[g], sem_follow, g, partner)

    def out_copy(g):
        at = pl.ds(pl.multiple_of(g * width, width), width)
        return pltpu.make_async_copy(out_ref.at[:, at], out_hbm.at[:, at], sem_out.at[g])

    def spill_copy(g):
        return remote(spill_out.at[g], spill_in.at[g], sem_spill, g, spill_to)

    rows = lax.broadcasted_iota(jnp.int32, (tokens, tokens), 0)
    cols = lax.broadcasted_iota(jnp.int32, (tokens, tokens), 1)
    tri = (rows >= cols).astype(jnp.float32)
    is_fwd = lax.broadcasted_iota(jnp.int32, (2 * PER, tokens), 0) < PER
    erow = lax.rem(lax.broadcasted_iota(jnp.int32, (4 * PER, width), 0), 2 * PER)
    ehead = lax.div(lax.broadcasted_iota(jnp.int32, (4 * PER, width), 1), HEADDIM)
    expand[0] = (erow == ehead + PER * (1 - d)).astype(jnp.float32).astype(jnp.bfloat16)
    expand[1] = (erow == ehead + PER * d).astype(jnp.float32).astype(jnp.bfloat16)
    for load in loads[:6]:
        load.wait()

    fold = BIG * reset_ref[...].astype(jnp.float32)

    @pl.when(index == 0)
    def _():
        halo_x[...] = jnp.zeros_like(halo_x)
        halo_bc[...] = jnp.zeros_like(halo_bc)
        span_in[...] = jnp.zeros_like(span_in)

    @pl.when(index > 0)
    def _():
        for copy in halos:
            copy.wait_recv()

    across = (((0,), (0,)), ((), ()))

    def hi_lo(v):
        hi = v.astype(jnp.bfloat16)
        lo = (v - hi.astype(jnp.float32)).astype(jnp.bfloat16)
        return jnp.concatenate([hi, lo], axis=0)

    def spread(v, which):
        return lax.dot_general(v, expand[which], across, preferred_element_type=jnp.float32)

    def spread_end(v, which):
        picked = expand[which, : 2 * PER].astype(jnp.float32) * v
        return jnp.broadcast_to(jnp.sum(picked, axis=0, keepdims=True), (8, width))

    def taps_of(ref, which, at):
        return [ref[k, which : which + 1, at] for k in range(4)]

    def relay(g):
        s_copy(g).wait_recv()
        t_copy(g).wait_recv()

        @pl.when(has_prev)
        def _():
            chain_copy(g).wait_recv()

        @pl.when(pos == 0)
        def _():
            chain_in[g] = jnp.zeros_like(chain_in[g])

        state = t_in[g][0:1] * chain_in[g].astype(jnp.float32) + s_in[g].astype(jnp.float32)

        @pl.when(has_next)
        def _():
            chain_out[g] = (t_own[g][0:1] * state + s_own[g]).astype(jnp.bfloat16)
            chain_copy(g).start()

        follow_copy(g).start()
        h_lead[g] = state.astype(jnp.bfloat16)

    @pl.loop(0, groups)
    def _(g):
        wide = pl.ds(pl.multiple_of(g * width, width), width)
        b_at = pl.ds(pl.multiple_of(g * STATE, STATE), STATE)
        c_at = pl.ds(pl.multiple_of((groups + g) * STATE, STATE), STATE)
        b_g = conv(halo_bc[:, b_at], bc_ref[:, b_at], taps_of(taps_bc, 0, b_at))
        bs[g] = b_g
        cs[g] = conv(halo_bc[:, c_at], bc_ref[:, c_at], taps_of(taps_bc, 1, b_at))
        heads = pl.ds(pl.multiple_of(g * PER, PER), PER)
        rate = jnp.concatenate([rate_ref[0, heads, :], rate_ref[1, heads, :]], axis=0)
        cum = lax.dot_general(rate * LOG2E - fold, tri, (((1,), (1,)), ((), ())),
                              precision=lax.Precision.HIGHEST, preferred_element_type=jnp.float32)
        r = -2.0 * rate
        small = r * (1.0 - r * (1 / 2 - r * (1 / 6 - r * (1 / 24 - r * (1 / 120 - r / 720)))))
        loss = jnp.where(r < 0.25, small, 1.0 - jnp.exp(-r))
        log_weight = jnp.maximum((0.5 * LOG2E) * jnp.log(loss), -1000.0)
        col = jnp.where(is_fwd, cum, -cum)
        row = log_weight - col
        colt[g] = col.T
        rowt[g] = row
        end = cum[:, tokens - 1 : tokens]
        to_end = hi_lo(jnp.exp2(row + jnp.where(is_fwd, end, 0.0)))
        lead_hl[g] = hi_lo(jnp.exp2(jnp.where(is_fwd, cum, end - cum)))
        total = jnp.exp2(end)
        x_g = conv(halo_x[:, wide], x_ref[:, wide], [taps_x[k : k + 1, wide] for k in range(4)])
        xc[g] = x_g
        xf = x_g.astype(jnp.float32)
        sent = (xf * spread(to_end, 1)).astype(jnp.bfloat16)
        state = lax.dot_general(b_g, sent, across, preferred_element_type=jnp.float32)
        ends = spread_end(total, 1)
        for k in range(2):
            s_send[2 * g + k] = state[:, k * part : (k + 1) * part].astype(jnp.bfloat16)
            t_send[2 * g + k] = ends[:, k * part : (k + 1) * part]
            s_copy(2 * g + k).start()
            t_copy(2 * g + k).start()
        kept = (xf * spread(to_end, 0)).astype(jnp.bfloat16)
        state = lax.dot_general(b_g, kept, across, preferred_element_type=jnp.float32)
        ends = spread_end(total, 0)
        for k in range(2):
            s_own[2 * g + k] = state[:, k * part : (k + 1) * part]
            t_own[2 * g + k] = ends[:, k * part : (k + 1) * part]

        @pl.when((pos == 0) & (g > 0))
        def _():
            relay(2 * g - 2)
            relay(2 * g - 1)

    slots = 4 * groups
    first = 7 * jnp.maximum(pos - 1, 0) - 4
    done_early = jnp.where(pos == 0, chunks - 2, jnp.where(pos == 1, 2, 0))
    done_before = jnp.where(pos == 0, chunks, jnp.clip(lax.div(slots - first + 2, 3), 0, chunks))

    @pl.when(pos == 0)
    def _():
        relay(chunks - 2)
        relay(chunks - 1)

    @pl.when(pos == 1)
    def _():
        relay(0)
        relay(1)

    left = lax.broadcasted_iota(jnp.int32, (tokens, 128), 1) < HEADDIM
    lower = rows[:half, :half] >= cols[:half, :half]

    @pl.loop(0, groups)
    def _(g):
        score = lax.dot_general(cs[g], bs[g], (((1,), (1,)), ((), ())), preferred_element_type=jnp.float32)
        for quarter in range(4):
            turn = 4 * g + quarter - first

            @pl.when((pos > 0) & (turn >= 0) & (lax.rem(turn, 3) == 0) & (lax.div(turn, 3) >= done_early) & (lax.div(turn, 3) < chunks))
            def _():
                relay(lax.div(turn, 3))

            for pair in range(quarter * PER // 8, (quarter + 1) * PER // 8):
                at = pair * 2 * HEADDIM
                x_pair = xc[g, :, at : at + 2 * HEADDIM]
                got = []
                for head in (2 * pair, 2 * pair + 1):
                    cf = colt[g, :, head : head + 1]
                    cb = colt[g, :, PER + head : PER + head + 1]
                    rf = rowt[g, head : head + 1, :]
                    rb = rowt[g, PER + head : PER + head + 1, :]
                    tl = jnp.where(lower, cf[:half] + rf[:, :half], cb[:half] + rb[:, :half])
                    tr = cb[:half] + rb[:, half:]
                    bl = cf[half:] + rf[:, :half]
                    br = jnp.where(lower, cf[half:] + rf[:, half:], cb[half:] + rb[:, half:])
                    top = jnp.concatenate([tl, tr], axis=1)
                    bottom = jnp.concatenate([bl, br], axis=1)
                    mix_top = (score[:half] * jnp.exp2(top)).astype(jnp.bfloat16)
                    mix_bottom = (score[half:] * jnp.exp2(bottom)).astype(jnp.bfloat16)
                    got.append(dot(jnp.concatenate([mix_top, mix_bottom], axis=0), x_pair))
                y_acc[g, :, at : at + 2 * HEADDIM] = jnp.where(left, got[0], got[1])

    for load in loads[6:]:
        load.wait()

    vis = span_ref.shape[1]
    token = index * tokens + lax.broadcasted_iota(jnp.int32, (tokens, vis), 0)

    def covers(ref):
        return ((token >= ref[0:1]) & (token < ref[1:2])).astype(jnp.float32).T

    inside = jnp.concatenate([covers(span_ref), covers(span_in)], axis=0).astype(jnp.bfloat16)
    same = lax.broadcasted_iota(jnp.int32, (vis, vis), 0) == lax.broadcasted_iota(jnp.int32, (vis, vis), 1)
    spanned = jnp.maximum(span_ref[1:2] - span_ref[0:1], 1).astype(jnp.float32)
    length = jnp.sum(jnp.where(same, spanned, 0.0), axis=1, keepdims=True)

    def skip_of(g):
        at = lax.broadcasted_iota(jnp.int32, (groups * PER, width), 0)
        head = lax.div(lax.broadcasted_iota(jnp.int32, (groups * PER, width), 1), HEADDIM)
        pick = (at == head + g * PER).astype(jnp.float32)
        skips = jnp.broadcast_to(skip_ref[...], (8, groups * PER))
        return lax.dot(skips, pick, precision=lax.Precision.HIGHEST,
                       preferred_element_type=jnp.float32)[0:1]

    @pl.loop(0, groups)
    def _(g):
        begin = jnp.where(g == 0, done_before, jnp.clip(jnp.maximum(2 * g, done_before + 2 * g), 0, chunks))
        finish = jnp.clip(done_before + 2 * g + 2, 0, chunks)

        @pl.when(begin < finish)
        def _():
            relay(begin)

        @pl.when(begin + 1 < finish)
        def _():
            relay(begin + 1)

        wide = pl.ds(pl.multiple_of(g * width, width), width)
        c_g = cs[g]
        lead = spread(lead_hl[g], 0) * dot(c_g, jnp.concatenate([h_lead[2 * g], h_lead[2 * g + 1]], axis=1))
        mixed = y_acc[g] + lead + skip_of(g) * xc[g].astype(jnp.float32)
        follow_copy(2 * g).wait_recv()
        follow_copy(2 * g + 1).wait_recv()
        mixed = mixed + spread(lead_hl[g], 1) * dot(c_g, jnp.concatenate([follow_in[2 * g], follow_in[2 * g + 1]], axis=1))
        gated = mixed * silu(gate_ref[:, wide].astype(jnp.float32))
        mean_sq = jnp.mean(gated * gated, axis=1, keepdims=True)
        token_out = (gated * lax.rsqrt(mean_sq + 1e-05) * gain_ref[:, wide]).astype(jnp.bfloat16)
        out_ref[:, wide] = token_out
        out_copy(g).start()
        sums = dot(inside, token_out)
        own_pool[g] = sums[:vis]
        spill_out[g] = sums[vis:]

        @pl.when(index > 0)
        def _():
            spill_copy(g).start()

    @pl.loop(0, groups)
    def _(g):
        wide = pl.ds(pl.multiple_of(g * width, width), width)

        @pl.when(index < last_index)
        def _():
            spill_copy(g).wait_recv()
            pool_ref[:, wide] = ((own_pool[g] + spill_in[g]) / length).astype(jnp.bfloat16)

        @pl.when(index == last_index)
        def _():
            pool_ref[:, wide] = (own_pool[g] / length).astype(jnp.bfloat16)

    @pl.loop(0, groups)
    def _(g):
        out_copy(g).wait()

    @pl.loop(0, chunks)
    def _(q):
        s_copy(q).wait_send()
        t_copy(q).wait_send()
        follow_copy(q).wait_send()

        @pl.when(has_next)
        def _():
            chain_copy(q).wait_send()

    @pl.when(index > 0)
    def _():
        @pl.loop(0, groups)
        def _(g):
            spill_copy(g).wait_send()

    @pl.when(index < last_index)
    def _():
        for copy in halos:
            copy.wait_send()


def on_device(
    x_in, bc_in, gate_z, log_decay, resets, conv_x, conv_bc, skip_d, norm_gain, visit_span
):
    tokens, channels = x_in.shape
    groups = bc_in.shape[2] // STATE
    width = PER * HEADDIM
    vis = visit_span.shape[0]

    f32, bf16 = jnp.float32, jnp.bfloat16
    state = (2 * groups, STATE, width // 2)
    ends = (2 * groups, 8, width // 2)
    whole = pl.BlockSpec(memory_space=pltpu.VMEM)
    outside = pl.BlockSpec(memory_space=pltpu.HBM)
    per_chunk = pltpu.SemaphoreType.DMA((2, 2 * groups))
    operands = (
        x_in,
        bc_in.reshape(tokens, 2 * groups * STATE),
        gate_z,
        log_decay.transpose(0, 2, 1),
        resets[None, :],
        conv_x,
        conv_bc,
        skip_d[None, :],
        norm_gain[None, :],
        visit_span.T,
    )
    return pl.pallas_call(
        functools.partial(kernel, lax.axis_size("ctx"), groups),
        out_shape=(
            jax.ShapeDtypeStruct((tokens, channels), bf16),
            jax.ShapeDtypeStruct((vis, channels), bf16),
        ),
        in_specs=[outside] * 10,
        out_specs=(outside, whole),
        scratch_shapes=[
            pltpu.VMEM((tokens, channels), bf16),
            *(pltpu.VMEM(v.shape, v.dtype) for v in operands),
            pltpu.VMEM((HALO, channels), bf16),
            pltpu.VMEM((HALO, 2 * groups * STATE), bf16),
            pltpu.VMEM((2, vis), jnp.int32),
            pltpu.VMEM((groups, tokens, width), bf16),
            pltpu.VMEM((groups, tokens, STATE), bf16),
            pltpu.VMEM((groups, tokens, STATE), bf16),
            pltpu.VMEM((groups, tokens, 2 * PER), f32),
            pltpu.VMEM((groups, 2 * PER, tokens), f32),
            pltpu.VMEM((groups, 4 * PER, tokens), bf16),
            pltpu.VMEM((2, 4 * PER, width), bf16),
            pltpu.VMEM((groups, tokens, width), f32),
            pltpu.VMEM(state, bf16),
            pltpu.VMEM(state, f32),
            pltpu.VMEM(ends, f32),
            pltpu.VMEM(state, bf16),
            pltpu.VMEM(ends, f32),
            pltpu.VMEM(state, bf16),
            pltpu.VMEM(ends, f32),
            pltpu.VMEM(state, bf16),
            pltpu.VMEM(state, bf16),
            pltpu.VMEM(state, bf16),
            pltpu.VMEM((groups, vis, width), f32),
            pltpu.VMEM((groups, vis, width), f32),
            pltpu.VMEM((groups, vis, width), f32),
            pltpu.SemaphoreType.DMA((10,)),
            pltpu.SemaphoreType.DMA((groups,)),
            pltpu.SemaphoreType.DMA((2, 3)),
            per_chunk, per_chunk, per_chunk, per_chunk,
            pltpu.SemaphoreType.DMA((2, groups)),
        ],
        compiler_params=pltpu.CompilerParams(
            collective_id=0, has_side_effects=True, vmem_limit_bytes=LIMIT << 20
        ),
    )(*operands)


def solution(mesh):
    return jax.shard_map(
        on_device,
        mesh=mesh,
        in_specs=(
            P(("groups", "ctx", "dp"), "tp"),
            P(("groups", "ctx", "dp"), None, "tp"),
            P(("groups", "ctx", "dp"), "tp"),
            P(None, ("groups", "ctx", "dp"), "tp"),
            P(("groups", "ctx", "dp")),
            P(None, "tp"),
            P(None, None, "tp"),
            P("tp"),
            P("tp"),
            P(("groups", "ctx", "dp"), None),
        ),
        out_specs=(P(("groups", "ctx", "dp"), "tp"), P(("groups", "ctx", "dp"), "tp")),
        check_vma=False,
    )
```
